512 devices in a mesh: tm: 8 (over y_lo, core), rows: 64 (over x, z, y_hi).
Axes of the slice: x: 4, y: 8 (y_hi: 2, y_lo: 4; y = y_hi * 4 + y_lo), z: 8, core: 2. Of those that a mesh axis runs over, the one named last changes fastest.
Arguments:
- inputs: bfloat16 [16, 256, 16, 256], P('tm', 'rows'), may hold values from -6 to 6
- cotangent: bfloat16 [16, 256, 16, 256], P('tm', 'rows'), may hold values from -16 to 16
- kernel: bfloat16 [27, 256, 256], P(None, 'rows', 'tm'), may hold values from -0.078125 to 0.078125
Outputs:
- grad_inputs: bfloat16 [16, 256, 16, 256], P('tm', 'rows')
- grad_kernel: float32 [27, 256, 256], P(None, 'rows', 'tm')
The draws below stay inside these ranges and needn't reach their ends.
All inputs are finite; a program needn't handle non-finite values.
Results may differ from the reference program's by a relative error of at most 0.003.
Values may be sent and summed in bfloat16 or wider, within the bound.
No kernel may reach another device: no remote copies, remote signals or barrier semaphores. Data moves between devices by JAX's collectives and lax.ppermute only.
A program may use at most 64 MiB of HBM per device.

```python
import jax
import jax.numpy as jnp
from jax import lax

C = 256
WIDTH = 16
FRAMES = 16
HEIGHT = 256


def raised(array, rng, source, target, shards_of, factor):
    owner, partner = [(jnp.arange(array.shape[dim]) // (array.shape[dim] // shards_of)).reshape([-1 if axis == dim else 1 for axis in range(array.ndim)]) for dim in (source, target)]
    chosen = jax.random.permutation(rng, shards_of)[partner]
    strong = (owner == chosen) | (owner == (partner + shards_of // 2) % shards_of)
    return jnp.where(strong, factor * array, array)


def block_scale(rng, dims, split, smallest, top_value):
    level, own = 1.0, jax.random.fold_in(rng, 6)
    for axis_at, parts in split:
        draws = jnp.exp(jax.random.uniform(jax.random.fold_in(own, axis_at), (parts,), jnp.float32, smallest / len(split), top_value / len(split)))
        level = level * jnp.repeat(draws, dims[axis_at] // parts).reshape([-1 if axis == axis_at else 1 for axis in range(len(dims))])
    return level


def bell_draw(stream_key, extent, scale, reach, cuts=(), kind=jnp.bfloat16):
    result = scale * jax.random.normal(stream_key, extent, jnp.float32)
    if cuts:
        result = result * block_scale(stream_key, extent, cuts, -0.22, 0.18)
    return jnp.clip(result, -reach, reach).astype(kind)


def bell_draw_with(stream_key, extent, deviation, limit, shards, heavy, dtype=jnp.bfloat16):
    entries = deviation * jax.random.normal(stream_key, extent, jnp.float32)
    if shards:
        entries = entries * block_scale(stream_key, extent, shards, -0.22, 0.18)
    return jnp.clip(raised(entries, jax.random.fold_in(stream_key, 3), *heavy), -limit, limit).astype(dtype)


def setup_inputs(seed: int = 0) -> dict:
    key_of = jax.random.split(jax.random.key(seed), 4)
    inputs = bell_draw(key_of[0], (FRAMES, HEIGHT, WIDTH, C), 1.0, 6.0, ((0, 8), (1, 64)))
    cotangent = bell_draw_with(key_of[1], (FRAMES, HEIGHT, WIDTH, C), 1.0, 16.0, ((0, 8), (1, 64)), (1, 3, 64, 4.0))
    kernel = bell_draw(key_of[2], (27, C, C), (27 * C) ** -0.5, 0.078125, ((1, 64), (2, 8)))
    return {"inputs": inputs, "cotangent": cotangent, "kernel": kernel}


def silu_slope(values):
    logistic = jax.nn.sigmoid(values)
    return logistic * (1.0 + values * (1.0 - logistic))

def convolve_back(gradient, kernel):
    frames, height, across, channels = gradient.shape
    padded = jnp.pad(gradient, ((0, 2), (1, 1), (1, 1), (0, 0)))
    summed = jnp.zeros((frames * height * across, kernel.shape[1]), jnp.float32)
    for time_tap in range(3):
        for row_tap in range(3):
            for col_tap in range(3):
                window = padded[2 - time_tap:2 - time_tap + frames, 2 - row_tap:2 - row_tap + height, 2 - col_tap:2 - col_tap + across].reshape(-1, channels)
                summed = summed + jnp.dot(window, kernel[9 * time_tap + 3 * row_tap + col_tap].T, preferred_element_type=jnp.float32)
    return summed.reshape(frames, height, across, -1)

def kernel_grad(source, gradient):
    frames, height, across, channels = source.shape
    padded = jnp.pad(source, ((2, 0), (1, 1), (1, 1), (0, 0)))
    flat_grad = gradient.reshape(-1, gradient.shape[3])
    pieces = []
    for time_tap in range(3):
        for row_tap in range(3):
            for col_tap in range(3):
                window = padded[time_tap:time_tap + frames, row_tap:row_tap + height, col_tap:col_tap + across].reshape(-1, channels)
                pieces.append(lax.dot_general(window, flat_grad, (((0,), (0,)), ((), ())), preferred_element_type=jnp.float32))
    return jnp.stack(pieces, 0)

def reference(inputs, cotangent, kernel):
    frames, height, across, channels = inputs.shape
    act = jax.nn.silu(inputs.astype(jnp.float32)).astype(jnp.bfloat16)
    grad_act = convolve_back(cotangent, kernel)
    grad_inputs = (cotangent.astype(jnp.float32) + grad_act * silu_slope(inputs.astype(jnp.float32))).astype(jnp.bfloat16)
    factor = float(frames * height * across) ** (-0.5)
    grad_kernel = kernel_grad(act, cotangent) * factor
    return (grad_inputs, grad_kernel)
```

```python
import jax
import jax.numpy as jnp
from jax import lax
from jax.sharding import PartitionSpec as P


def silu_slope(values):
    logistic = jax.nn.sigmoid(values)
    return logistic * (1.0 + values * (1.0 - logistic))


def exchanged(blocks, axis):
    return lax.all_to_all(blocks, axis, split_axis=0, concat_axis=0, tiled=True)


def with_halo_rows(block):
    count = lax.axis_size("rows")
    forward = [(i, i + 1) for i in range(count - 1)]
    backward = [(target, source) for source, target in forward]
    above = lax.ppermute(block[:, -1:], "rows", forward)
    below = lax.ppermute(block[:, :1], "rows", backward)
    return jnp.concatenate([above, block, below], axis=1)


def tap_windows(padded, frames, height, across):
    pieces = [
        padded[2 - t : 2 - t + frames, 2 - r : 2 - r + height, 2 - c : 2 - c + across]
        for t in range(3)
        for r in range(3)
        for c in range(3)
    ]
    return jnp.concatenate(pieces, axis=3)


def local(inputs, cotangent, kernel):
    frames, height, across, channels = inputs.shape
    groups = lax.axis_size("tm")
    bands = lax.axis_size("rows")
    taps, own_in, own_out = kernel.shape
    points = frames * height * across

    own_kernel = jnp.transpose(kernel, (1, 0, 2)).reshape(1, own_in, taps * own_out)
    kernel_in = exchanged(jnp.broadcast_to(own_kernel, (bands, own_in, taps * own_out)), "rows")
    kernel_in = kernel_in.reshape(bands * own_in, taps * own_out)

    act = jax.nn.silu(inputs.astype(jnp.float32)).astype(jnp.bfloat16)
    act_all = lax.all_gather(act.reshape(points, channels), "tm", axis=0, tiled=True)

    haloed = with_halo_rows(cotangent)
    split = haloed.reshape(frames, height + 2, across, groups, own_out).transpose(3, 0, 1, 2, 4)
    grads = exchanged(split, "tm").reshape(groups * frames, height + 2, across, own_out)
    padded = jnp.pad(grads, ((0, 2), (0, 0), (1, 1), (0, 0)))
    windows = tap_windows(padded, groups * frames, height, across)
    windows = windows.reshape(groups * points, taps * own_out)

    factor = float(points * groups * bands) ** (-0.5)
    terms = lax.dot_general(
        act_all, windows, (((0,), (0,)), ((), ())), preferred_element_type=jnp.float32
    )
    terms = (terms * factor).astype(jnp.bfloat16).reshape(bands, own_in, taps * own_out)
    grad_kernel = jnp.sum(exchanged(terms, "rows").astype(jnp.float32), axis=0)
    grad_kernel = grad_kernel.reshape(own_in, taps, own_out).transpose(1, 0, 2)

    partial = lax.dot_general(
        windows, kernel_in, (((1,), (1,)), ((), ())), preferred_element_type=jnp.float32
    )
    partial = partial.astype(jnp.bfloat16).reshape(groups, points, channels)
    grad_act = jnp.sum(exchanged(partial, "tm").astype(jnp.float32), axis=0)
    grad_act = grad_act.reshape(inputs.shape)
    grad_inputs = (
        cotangent.astype(jnp.float32) + grad_act * silu_slope(inputs.astype(jnp.float32))
    ).astype(jnp.bfloat16)
    return (grad_inputs, grad_kernel)


def solution(mesh):
    return jax.shard_map(
        local,
        mesh=mesh,
        in_specs=(P("tm", "rows", None, None), P("tm", "rows", None, None), P(None, "rows", "tm")),
        out_specs=(P("tm", "rows", None, None), P(None, "rows", "tm")),
        check_vma=False,
    )
```

```python
import jax
import jax.numpy as jnp
from jax import lax
from jax.experimental import pallas as pl
from jax.experimental.pallas import tpu as pltpu
from jax.sharding import PartitionSpec as P


BF16 = jnp.bfloat16
F32 = jnp.float32
CHIPS = 4
CORES = 2
GROUPS = CHIPS * CORES
FAR = 4
OWN = 32
TAPS = 27
LANES = 128
SLOT = 896
WIDE = 9 * LANES


def chip_and_core():
    me = lax.axis_index("tm")
    return me // CORES, me % CORES


def called(body, outs, *args, scratch=(), flops=0, limit=24):
    whole = pl.BlockSpec(memory_space=pltpu.VMEM)
    size = sum(a.size * a.dtype.itemsize for a in (*args, *outs))
    return pl.pallas_call(
        body,
        out_shape=outs,
        in_specs=[whole] * len(args),
        out_specs=[whole] * len(outs),
        scratch_shapes=scratch,
        compiler_params=pltpu.CompilerParams(vmem_limit_bytes=limit << 20),
        cost_estimate=pl.CostEstimate(flops=flops, bytes_accessed=size, transcendentals=0),
    )(*args)


def array(shape, dtype=BF16):
    return jax.ShapeDtypeStruct(shape, dtype)


def prepare(kernel_ref, inputs_ref, cot_ref, blocks_ref, above_ref, below_ref, body_ref):
    own_in = kernel_ref.shape[1]
    _, channels = inputs_ref.shape[2:]
    above_ref[...] = cot_ref[:, cot_ref.shape[1] - 1]
    below_ref[...] = cot_ref[:, 0]
    body_ref[:, :channels] = jnp.broadcast_to(
        jax.nn.silu(inputs_ref[...].reshape(-1, channels).astype(F32)).T.astype(BF16)[None],
        (CHIPS, channels, LANES),
    )
    halves = [cot_ref[frame].reshape(-1, channels).astype(F32) for frame in range(2)]
    for target in range(CHIPS):
        body_ref[target, channels:] = for_chip(target, *halves)
    pieces = [kernel_ref[tap].astype(F32) for tap in range(TAPS)]
    pieces.append(jnp.zeros((own_in, SLOT - TAPS * OWN), F32))
    slot = jnp.concatenate(pieces, axis=1).astype(BF16)
    blocks_ref[...] = jnp.broadcast_to(slot[None], blocks_ref.shape)


def for_chip(target, first, second):
    tile = slice(LANES * (target // 2), LANES * (target // 2) + LANES)
    first, second = first[:, tile], second[:, tile]
    low = lax.broadcasted_iota(jnp.int32, first.shape, 1) < LANES // 2
    if target % 2 == 0:
        second = pltpu.roll(second, LANES // 2, 1)
    else:
        first = pltpu.roll(first, LANES // 2, 1)
    return jnp.where(low, first, second).astype(BF16)


def pack(body_ref, above_ref, below_ref, *out_and_scratch):
    outs, halo = out_and_scratch[:CHIPS], out_and_scratch[CHIPS]
    chip, _ = chip_and_core()
    rows = body_ref.shape[1]
    across = above_ref.shape[1]
    for side, ref in enumerate((above_ref, below_ref)):
        halves = [ref[frame].astype(F32) for frame in range(2)]
        for target in range(CHIPS):
            halo[target, across * side : across * side + across] = for_chip(target, *halves)
    for step, out in enumerate(outs):
        out[:rows] = body_ref[chip ^ step]
        out[rows:] = halo[chip ^ step]


def windows_and_terms(factor, all_ref, terms_ref, windows_ref, act, padded):
    chip, core = chip_and_core()
    channels = act.shape[0]
    across = 16
    height = 4
    span = (height + 2) * across
    row = lax.broadcasted_iota(jnp.int32, (LANES, LANES), 0)
    lane = lax.broadcasted_iota(jnp.int32, (LANES, LANES), 1)
    place = lax.broadcasted_iota(jnp.int32, (span, LANES), 0) % across
    group = lax.broadcasted_iota(jnp.int32, (span, LANES), 1) // OWN
    padded[2 * GROUPS :] = jnp.zeros((2, span, LANES), BF16)
    for other in range(CORES):
        for step in range(CHIPS):
            owner = CORES * (chip ^ step) + other
            act[:, pl.ds(pl.multiple_of(owner * LANES, LANES), LANES)] = all_ref[other, step, :channels]
            block = all_ref[other, step, channels:]
            held = span - 2 * across
            block = jnp.concatenate([block[held : held + across], block[:held], block[held + across :]], axis=0)
            for frame in range(2):
                chosen = (row == 64 * frame + OWN * core + lane % OWN).astype(F32).astype(BF16)
                copies = jnp.dot(block, chosen, preferred_element_type=F32)
                after = jnp.where(place == across - 1, 0.0, pltpu.roll(copies, span - 1, 0))
                before = jnp.where(place == 0, 0.0, pltpu.roll(copies, 1, 0))
                joined = jnp.where(group == 0, after, jnp.where(group == 1, copies, before))
                joined = jnp.where(group == 3, 0.0, joined)
                padded[CORES * owner + frame] = joined.astype(BF16)
    for time_tap in range(3):
        for row_tap in range(3):
            part = padded[2 - time_tap : 2 - time_tap + 2 * GROUPS, across * (2 - row_tap) : across * (2 - row_tap + height)]
            index = 3 * time_tap + row_tap
            windows_ref[:, LANES * index : LANES * index + LANES] = part.reshape(-1, LANES)
    terms = jnp.dot(act[...], windows_ref[...], preferred_element_type=F32) * factor
    pieces = [terms[:, LANES * index : LANES * index + 3 * OWN] for index in range(9)]
    pieces.append(jnp.zeros((channels, SLOT - TAPS * OWN), F32))
    terms = jnp.concatenate(pieces, axis=1)
    terms_ref[...] = terms.reshape(terms_ref.shape).astype(BF16)


def transposed(windows_ref, kernel_ref, keep_ref, give_ref, wide, product):
    chip, core = chip_and_core()
    bands, own_in, _ = kernel_ref.shape
    flat = kernel_ref[...].astype(F32).reshape(bands * own_in, SLOT)
    for index in range(9):
        wide[:, LANES * index : LANES * index + LANES] = flat[:, 3 * OWN * index : 3 * OWN * index + LANES].astype(BF16)
    product[...] = lax.dot_general(
        windows_ref[...], wide[...], (((1,), (1,)), ((), ())), preferred_element_type=F32
    ).reshape(product.shape)
    for step in range(CHIPS):
        keep_ref[step] = product[CORES * (chip ^ step) + core]
        give_ref[step] = product[CORES * (chip ^ step) + 1 - core].astype(BF16)


def paired(keep_ref, given_ref, own_ref, *outs):
    own_ref[...] = keep_ref[0] + given_ref[0].astype(F32)
    for step, out in enumerate(outs, 1):
        out[...] = (keep_ref[step] + given_ref[step].astype(F32)).astype(BF16)


def finish(own_ref, first_ref, second_ref, third_ref, inputs_ref, cot_ref, out_ref):
    total = own_ref[...] + first_ref[...].astype(F32) + second_ref[...].astype(F32) + third_ref[...].astype(F32)
    total = total.reshape(inputs_ref.shape)
    values = inputs_ref[...].astype(F32)
    logistic = jax.nn.sigmoid(values)
    slope = logistic * (1.0 + values * (1.0 - logistic))
    out_ref[...] = (cot_ref[...].astype(F32) + total * slope).astype(BF16)


def summed(terms_ref, out_ref):
    total = jnp.sum(terms_ref[...].astype(F32), axis=0)
    for tap in range(TAPS):
        out_ref[tap] = total[:, OWN * tap : OWN * tap + OWN]


def stepped(block, step):
    count = GROUPS
    return lax.ppermute(block, "tm", [(i, i ^ step) for i in range(count)])


def near_and_far(bands):
    near = bands // FAR
    return (
        [[near * x + i for i in range(near)] for x in range(FAR)],
        [[near * x + i for x in range(FAR)] for i in range(near)],
    )


def exchanged(blocks, groups):
    return lax.all_to_all(
        blocks, "rows", split_axis=0, concat_axis=0, tiled=True, axis_index_groups=groups
    )


def local(inputs, cotangent, kernel):
    frames, height, across, channels = inputs.shape
    bands = lax.axis_size("rows")
    own_in = kernel.shape[1]
    points = frames * height * across

    held = height * across
    blocks, above, below, body = called(
        prepare,
        [
            array((bands // FAR, own_in, SLOT)), array((frames, across, channels)),
            array((frames, across, channels)), array((CHIPS, channels + held, LANES)),
        ],
        kernel, inputs, cotangent, limit=60,
    )
    forward = [(i, i + 1) for i in range(bands - 1)]
    above = lax.ppermute(above, "rows", forward)
    below = lax.ppermute(below, "rows", [(b, a) for a, b in forward])

    near, far = near_and_far(bands)
    blocks = exchanged(blocks, near)
    blocks = jnp.broadcast_to(blocks[None], (FAR, *blocks.shape))
    kernel_in = exchanged(blocks, far).reshape(bands, own_in, SLOT)

    span = (height + 2) * across
    payload = array((channels + span, LANES))
    packs = called(
        pack, [payload] * CHIPS, body, above, below,
        scratch=[pltpu.VMEM((CHIPS, 2 * across, LANES), BF16)],
    )
    packs = [packs[0]] + [stepped(packs[step], CORES * step) for step in range(1, CHIPS)]
    every = lax.all_gather(jnp.stack(packs), "tm", axis=0, axis_index_groups=[[2 * i, 2 * i + 1] for i in range(CHIPS)])

    factor = float(points * GROUPS * bands) ** (-0.5)

    def terms_body(*refs):
        windows_and_terms(factor, *refs)

    terms, windows = called(
        terms_body, [array((bands, own_in, SLOT)), array((GROUPS * points, WIDE))], every,
        scratch=[pltpu.VMEM((channels, GROUPS * points), BF16), pltpu.VMEM((frames * GROUPS + 2, span, LANES), BF16)],
        flops=2 * GROUPS * points * WIDE * channels,
    )
    terms = exchanged(terms, None)

    keep, give = called(
        transposed, [array((CHIPS, points, channels), F32), array((CHIPS, points, channels))],
        windows, kernel_in,
        scratch=[pltpu.VMEM((channels, WIDE), BF16), pltpu.VMEM((GROUPS, points, channels), F32)],
        flops=2 * GROUPS * points * WIDE * channels,
    )
    given = stepped(give, 1)
    own, *sums = called(
        paired, [array((points, channels), F32)] + [array((points, channels))] * 3, keep, given
    )
    sums = [stepped(part, CORES * step) for step, part in enumerate(sums, 1)]
    grad_inputs, = called(finish, [array(inputs.shape)], own, *sums, inputs, cotangent)
    grad_kernel, = called(summed, [array(kernel.shape, F32)], terms)
    return (grad_inputs, grad_kernel)


def solution(mesh):
    return jax.shard_map(
        local,
        mesh=mesh,
        in_specs=(P("tm", "rows", None, None), P("tm", "rows", None, None), P(None, "rows", "tm")),
        out_specs=(P("tm", "rows", None, None), P(None, "rows", "tm")),
        check_vma=False,
    )
```

```python
import jax
import jax.numpy as jnp
from jax import lax
from jax.experimental import pallas as pl
from jax.experimental.pallas import tpu as pltpu
from jax.sharding import PartitionSpec as P


BF16 = jnp.bfloat16
F32 = jnp.float32
CHIPS = 4
CORES = 2
GROUPS = CHIPS * CORES
PAIRS = [[CORES * chip + core for core in range(CORES)] for chip in range(CHIPS)]
FAR = 4
OWN = 32
TAPS = 27
LANES = 128
SLOT = 896
WIDE = 9 * LANES


def chip_and_core():
    me = lax.axis_index("tm")
    return me // CORES, me % CORES


def called(body, outs, *args, scratch=(), flops=0, limit=24):
    whole = pl.BlockSpec(memory_space=pltpu.VMEM)
    size = sum(a.size * a.dtype.itemsize for a in (*args, *outs))
    return pl.pallas_call(
        body,
        out_shape=outs,
        in_specs=[whole] * len(args),
        out_specs=[whole] * len(outs),
        scratch_shapes=scratch,
        compiler_params=pltpu.CompilerParams(vmem_limit_bytes=limit << 20),
        cost_estimate=pl.CostEstimate(flops=flops, bytes_accessed=size, transcendentals=0),
    )(*args)


def array(shape, dtype=BF16):
    return jax.ShapeDtypeStruct(shape, dtype)


def prepare(kernel_ref, inputs_ref, cot_ref, swap_ref, second_ref, body_ref):
    own_in = kernel_ref.shape[1]
    across, channels = inputs_ref.shape[2:]
    odd = lax.axis_index("rows") % 2
    last = cot_ref.shape[1] - 1
    for ref, row in ((swap_ref, (1 - odd) * last), (second_ref, odd * last)):
        for frame in range(2):
            values = cot_ref[frame, row]
            for tile in range(2):
                start = across * (2 * frame + tile)
                ref[start : start + across] = values[:, LANES * tile : LANES * tile + LANES]
    pieces = [kernel_ref[tap].astype(F32) for tap in range(TAPS)]
    pieces.append(jnp.zeros((own_in, SLOT - TAPS * OWN), F32))
    slot = jnp.concatenate(pieces, axis=1)
    tiles = [slot[:, start : start + LANES] for start in range(0, SLOT, LANES)]
    tiles.append(jnp.zeros((swap_ref.shape[0] - 4 * across - SLOT // LANES * own_in, LANES), F32))
    swap_ref[4 * across :] = jnp.concatenate(tiles, axis=0).astype(BF16)
    body_ref[:, :channels] = jnp.broadcast_to(
        jax.nn.silu(inputs_ref[...].reshape(-1, channels).astype(F32)).T.astype(BF16)[None],
        (CHIPS, channels, LANES),
    )
    halves = [cot_ref[frame].reshape(-1, channels).astype(F32) for frame in range(2)]
    for target in range(CHIPS):
        body_ref[target, channels:] = for_chip(target, halves[0], halves[1])


def joined(own_ref, swapped_ref, blocks_ref):
    own_in = blocks_ref.shape[2]
    start = own_ref.shape[0] - LANES // 4
    odd = lax.axis_index("rows") % 2
    for place, ref in ((odd, own_ref), (1 - odd, swapped_ref)):
        values = ref[start:].astype(F32)
        tiles = [values[own_in * tile : own_in * tile + own_in] for tile in range(SLOT // LANES)]
        slot = jnp.concatenate(tiles, axis=1).astype(BF16)
        for pair in range(blocks_ref.shape[0]):
            blocks_ref[pair, place] = slot


def for_chip(target, first, second):
    tile = slice(LANES * (target // 2), LANES * (target // 2) + LANES)
    return halved(target, first[:, tile], second[:, tile])


def halved(target, first, second):
    low = lax.broadcasted_iota(jnp.int32, first.shape, 1) < LANES // 2
    if target % 2 == 0:
        second = pltpu.roll(second, LANES // 2, 1)
    else:
        first = pltpu.roll(first, LANES // 2, 1)
    return jnp.where(low, first, second).astype(BF16)


def pack(body_ref, first_ref, second_ref, *out_and_scratch):
    outs, halo = out_and_scratch[:CHIPS], out_and_scratch[CHIPS]
    chip, _ = chip_and_core()
    rows = body_ref.shape[1]
    across = 16
    odd = lax.axis_index("rows") % 2
    for side, ref in ((1 - odd, first_ref), (odd, second_ref)):
        tiles = [ref[across * tile : across * tile + across].astype(F32) for tile in range(4)]
        for target in range(CHIPS):
            tile = target // 2
            part = halved(target, tiles[tile], tiles[2 + tile])
            halo[target, pl.ds(pl.multiple_of(across * side, across), across)] = part
    for step, out in enumerate(outs):
        out[:rows] = body_ref[chip ^ step]
        out[rows:] = halo[chip ^ step]


def windows_and_terms(factor, all_ref, terms_ref, windows_ref, act, padded):
    chip, core = chip_and_core()
    channels = act.shape[0]
    across = 16
    height = 4
    span = (height + 2) * across
    row = lax.broadcasted_iota(jnp.int32, (LANES, LANES), 0)
    lane = lax.broadcasted_iota(jnp.int32, (LANES, LANES), 1)
    place = lax.broadcasted_iota(jnp.int32, (span, LANES), 0) % across
    group = lax.broadcasted_iota(jnp.int32, (span, LANES), 1) // OWN
    padded[2 * GROUPS :] = jnp.zeros((2, span, LANES), BF16)
    for other in range(CORES):
        for step in range(CHIPS):
            owner = CORES * (chip ^ step) + other
            act[:, pl.ds(pl.multiple_of(owner * LANES, LANES), LANES)] = all_ref[other, step, :channels]
            block = all_ref[other, step, channels:]
            held = span - 2 * across
            block = jnp.concatenate([block[held : held + across], block[:held], block[held + across :]], axis=0)
            for frame in range(2):
                chosen = (row == 64 * frame + OWN * core + lane % OWN).astype(F32).astype(BF16)
                copies = jnp.dot(block, chosen, preferred_element_type=F32)
                after = jnp.where(place == across - 1, 0.0, pltpu.roll(copies, span - 1, 0))
                before = jnp.where(place == 0, 0.0, pltpu.roll(copies, 1, 0))
                joined = jnp.where(group == 0, after, jnp.where(group == 1, copies, before))
                joined = jnp.where(group == 3, 0.0, joined)
                padded[CORES * owner + frame] = joined.astype(BF16)
    for time_tap in range(3):
        for row_tap in range(3):
            part = padded[2 - time_tap : 2 - time_tap + 2 * GROUPS, across * (2 - row_tap) : across * (2 - row_tap + height)]
            index = 3 * time_tap + row_tap
            windows_ref[:, LANES * index : LANES * index + LANES] = part.reshape(-1, LANES)
    terms = jnp.dot(act[...], windows_ref[...], preferred_element_type=F32) * factor
    pieces = [terms[:, LANES * index : LANES * index + 3 * OWN] for index in range(9)]
    pieces.append(jnp.zeros((channels, SLOT - TAPS * OWN), F32))
    terms = jnp.concatenate(pieces, axis=1)
    terms_ref[...] = terms.reshape(terms_ref.shape).astype(BF16)


def transposed(windows_ref, kernel_ref, keep_ref, give_ref, wide, product):
    chip, core = chip_and_core()
    bands, own_in, _ = kernel_ref.shape
    flat = kernel_ref[...].astype(F32).reshape(bands * own_in, SLOT)
    for index in range(9):
        wide[:, LANES * index : LANES * index + LANES] = flat[:, 3 * OWN * index : 3 * OWN * index + LANES].astype(BF16)
    product[...] = lax.dot_general(
        windows_ref[...], wide[...], (((1,), (1,)), ((), ())), preferred_element_type=F32
    ).reshape(product.shape)
    for step in range(CHIPS):
        keep_ref[step] = product[CORES * (chip ^ step) + core]
        give_ref[step] = product[CORES * (chip ^ step) + 1 - core].astype(BF16)


def paired(keep_ref, given_ref, own_ref, *outs):
    own_ref[...] = keep_ref[0] + given_ref[0].astype(F32)
    for step, out in enumerate(outs, 1):
        out[...] = (keep_ref[step] + given_ref[step].astype(F32)).astype(BF16)


def finish(own_ref, first_ref, second_ref, third_ref, inputs_ref, cot_ref, out_ref):
    total = own_ref[...] + first_ref[...].astype(F32) + second_ref[...].astype(F32) + third_ref[...].astype(F32)
    total = total.reshape(inputs_ref.shape)
    values = inputs_ref[...].astype(F32)
    logistic = jax.nn.sigmoid(values)
    slope = logistic * (1.0 + values * (1.0 - logistic))
    out_ref[...] = (cot_ref[...].astype(F32) + total * slope).astype(BF16)


def summed(terms_ref, out_ref):
    total = jnp.sum(terms_ref[...].astype(F32), axis=0)
    for tap in range(TAPS):
        out_ref[tap] = total[:, OWN * tap : OWN * tap + OWN]


def stepped(block, step):
    count = GROUPS
    return lax.ppermute(block, "tm", [(i, i ^ step) for i in range(count)])


def near_and_far(bands):
    near = bands // FAR
    return (
        [[near * x + 2 * i + odd for i in range(near // 2)] for x in range(FAR) for odd in range(2)],
        [[near * x + i for x in range(FAR)] for i in range(near)],
    )


def exchanged(blocks, groups):
    return lax.all_to_all(
        blocks, "rows", split_axis=0, concat_axis=0, tiled=True, axis_index_groups=groups
    )


def local(inputs, cotangent, kernel):
    frames, height, across, channels = inputs.shape
    bands = lax.axis_size("rows")
    own_in = kernel.shape[1]
    points = frames * height * across

    held = height * across
    swap, second, body = called(
        prepare,
        [
            array((4 * across + LANES // 4, LANES)), array((4 * across, LANES)),
            array((CHIPS, channels + held, LANES)),
        ],
        kernel, inputs, cotangent, limit=60,
    )
    first = lax.ppermute(swap, "rows", [(i, i ^ 1) for i in range(bands)])
    pairs = [(i, i + 1) for i in range(1, bands - 1, 2)]
    second = lax.ppermute(second, "rows", pairs + [(b, a) for a, b in pairs])
    blocks, = called(joined, [array((bands // FAR // 2, 2, own_in, SLOT))], swap, first)

    near, far = near_and_far(bands)
    blocks = exchanged(blocks, near)
    blocks = blocks.reshape(bands // FAR, own_in, SLOT)
    blocks = jnp.broadcast_to(blocks[None], (FAR, *blocks.shape))
    kernel_in = exchanged(blocks, far).reshape(bands, own_in, SLOT)

    span = (height + 2) * across
    payload = array((channels + span, LANES))
    packs = called(
        pack, [payload] * CHIPS, body, first, second,
        scratch=[pltpu.VMEM((CHIPS, 2 * across, LANES), BF16)],
    )
    packs = [packs[0]] + [stepped(packs[step], CORES * step) for step in range(1, CHIPS)]
    every = lax.all_gather(
        jnp.stack(packs), "tm", axis=0, axis_index_groups=PAIRS
    )

    factor = float(points * GROUPS * bands) ** (-0.5)

    def terms_body(*refs):
        windows_and_terms(factor, *refs)

    terms, windows = called(
        terms_body, [array((bands, own_in, SLOT)), array((GROUPS * points, WIDE))], every,
        scratch=[pltpu.VMEM((channels, GROUPS * points), BF16), pltpu.VMEM((frames * GROUPS + 2, span, LANES), BF16)],
        flops=2 * GROUPS * points * WIDE * channels,
    )
    terms = exchanged(terms, None)

    keep, give = called(
        transposed, [array((CHIPS, points, channels), F32), array((CHIPS, points, channels))],
        windows, kernel_in,
        scratch=[pltpu.VMEM((channels, WIDE), BF16), pltpu.VMEM((GROUPS, points, channels), F32)],
        flops=2 * GROUPS * points * WIDE * channels,
    )
    given = stepped(give, 1)
    own, *sums = called(
        paired, [array((points, channels), F32)] + [array((points, channels))] * 3, keep, given
    )
    sums = [stepped(part, CORES * step) for step, part in enumerate(sums, 1)]
    grad_inputs, = called(finish, [array(inputs.shape)], own, *sums, inputs, cotangent)
    grad_kernel, = called(summed, [array(kernel.shape, F32)], terms)
    return (grad_inputs, grad_kernel)


def solution(mesh):
    return jax.shard_map(
        local,
        mesh=mesh,
        in_specs=(P("tm", "rows", None, None), P("tm", "rows", None, None), P(None, "rows", "tm")),
        out_specs=(P("tm", "rows", None, None), P(None, "rows", "tm")),
        check_vma=False,
    )
```

```python
import jax
import jax.numpy as jnp
from jax import lax
from jax.experimental import pallas as pl
from jax.experimental.pallas import tpu as pltpu
from jax.sharding import PartitionSpec as P


BF16 = jnp.bfloat16
F32 = jnp.float32
CHIPS = 4
CORES = 2
GROUPS = CHIPS * CORES
PAIRS = [[CORES * chip + core for core in range(CORES)] for chip in range(CHIPS)]
FAR = 4
OWN = 32
TAPS = 27
LANES = 128
SLOT = 896
WIDE = 9 * LANES


def chip_and_core():
    me = lax.axis_index("tm")
    return me // CORES, me % CORES


def called(body, outs, *args, scratch=(), flops=0, limit=24):
    whole = pl.BlockSpec(memory_space=pltpu.VMEM)
    size = sum(a.size * a.dtype.itemsize for a in (*args, *outs))
    return pl.pallas_call(
        body,
        out_shape=outs,
        in_specs=[whole] * len(args),
        out_specs=[whole] * len(outs),
        scratch_shapes=scratch,
        compiler_params=pltpu.CompilerParams(vmem_limit_bytes=limit << 20),
        cost_estimate=pl.CostEstimate(flops=flops, bytes_accessed=size, transcendentals=0),
    )(*args)


def array(shape, dtype=BF16):
    return jax.ShapeDtypeStruct(shape, dtype)


def prepare(kernel_ref, inputs_ref, cot_ref, swap_ref, second_ref, body_ref):
    own_in = kernel_ref.shape[1]
    across, channels = inputs_ref.shape[2:]
    odd = lax.axis_index("rows") % 2
    last = cot_ref.shape[1] - 1
    for ref, row in ((swap_ref, (1 - odd) * last), (second_ref, odd * last)):
        for frame in range(2):
            values = cot_ref[frame, row]
            for tile in range(2):
                start = across * (2 * frame + tile)
                ref[start : start + across] = values[:, LANES * tile : LANES * tile + LANES]
    pieces = [kernel_ref[tap].astype(F32) for tap in range(TAPS)]
    pieces.append(jnp.zeros((own_in, SLOT - TAPS * OWN), F32))
    slot = jnp.concatenate(pieces, axis=1)
    tiles = [slot[:, start : start + LANES] for start in range(0, SLOT, LANES)]
    tiles.append(jnp.zeros((swap_ref.shape[0] - 4 * across - SLOT // LANES * own_in, LANES), F32))
    swap_ref[4 * across :] = jnp.concatenate(tiles, axis=0).astype(BF16)
    body_ref[:channels] = jax.nn.silu(inputs_ref[...].reshape(-1, channels).astype(F32)).T.astype(BF16)
    halves = [cot_ref[frame].reshape(-1, channels).astype(F32) for frame in range(2)]
    for target in range(CHIPS):
        part = for_chip(target, halves[0], halves[1])
        body_ref[channels + part.shape[0] * target : channels + part.shape[0] * (target + 1)] = part


def joined(own_ref, swapped_ref, blocks_ref):
    own_in = blocks_ref.shape[2]
    start = own_ref.shape[0] - LANES // 4
    odd = lax.axis_index("rows") % 2
    for place, ref in ((odd, own_ref), (1 - odd, swapped_ref)):
        values = ref[start:].astype(F32)
        tiles = [values[own_in * tile : own_in * tile + own_in] for tile in range(SLOT // LANES)]
        slot = jnp.concatenate(tiles, axis=1).astype(BF16)
        for pair in range(blocks_ref.shape[0]):
            blocks_ref[pair, place] = slot


def for_chip(target, first, second):
    tile = slice(LANES * (target // 2), LANES * (target // 2) + LANES)
    return halved(target, first[:, tile], second[:, tile])


def halved(target, first, second):
    low = lax.broadcasted_iota(jnp.int32, first.shape, 1) < LANES // 2
    if target % 2 == 0:
        second = pltpu.roll(second, LANES // 2, 1)
    else:
        first = pltpu.roll(first, LANES // 2, 1)
    return jnp.where(low, first, second).astype(BF16)


def pack(body_ref, first_ref, second_ref, *out_and_scratch):
    outs, halo = out_and_scratch[:CHIPS], out_and_scratch[CHIPS]
    chip, _ = chip_and_core()
    across = 16
    rows = outs[0].shape[0] - 2 * across
    channels = 256
    held = rows - channels
    odd = lax.axis_index("rows") % 2
    for side, ref in ((1 - odd, first_ref), (odd, second_ref)):
        tiles = [ref[across * tile : across * tile + across].astype(F32) for tile in range(4)]
        for target in range(CHIPS):
            tile = target // 2
            part = halved(target, tiles[tile], tiles[2 + tile])
            halo[target, pl.ds(pl.multiple_of(across * side, across), across)] = part
    for step, out in enumerate(outs):
        out[:channels] = body_ref[:channels]
        start = pl.multiple_of(channels + held * (chip ^ step), held)
        out[channels:rows] = body_ref[pl.ds(start, held)]
        out[rows:] = halo[chip ^ step]


def windows_and_terms(factor, all_ref, terms_ref, windows_ref, act, padded):
    chip, core = chip_and_core()
    channels = act.shape[0]
    across = 16
    height = 4
    span = (height + 2) * across
    row = lax.broadcasted_iota(jnp.int32, (LANES, LANES), 0)
    lane = lax.broadcasted_iota(jnp.int32, (LANES, LANES), 1)
    place = lax.broadcasted_iota(jnp.int32, (span, LANES), 0) % across
    group = lax.broadcasted_iota(jnp.int32, (span, LANES), 1) // OWN
    padded[2 * GROUPS :] = jnp.zeros((2, span, LANES), BF16)
    for other in range(CORES):
        for step in range(CHIPS):
            owner = CORES * (chip ^ step) + other
            act[:, pl.ds(pl.multiple_of(owner * LANES, LANES), LANES)] = all_ref[other, step, :channels]
            block = all_ref[other, step, channels:]
            held = span - 2 * across
            block = jnp.concatenate([block[held : held + across], block[:held], block[held + across :]], axis=0)
            for frame in range(2):
                chosen = (row == 64 * frame + OWN * core + lane % OWN).astype(F32).astype(BF16)
                copies = jnp.dot(block, chosen, preferred_element_type=F32)
                after = jnp.where(place == across - 1, 0.0, pltpu.roll(copies, span - 1, 0))
                before = jnp.where(place == 0, 0.0, pltpu.roll(copies, 1, 0))
                joined = jnp.where(group == 0, after, jnp.where(group == 1, copies, before))
                joined = jnp.where(group == 3, 0.0, joined)
                padded[CORES * owner + frame] = joined.astype(BF16)
    for time_tap in range(3):
        for row_tap in range(3):
            part = padded[2 - time_tap : 2 - time_tap + 2 * GROUPS, across * (2 - row_tap) : across * (2 - row_tap + height)]
            index = 3 * time_tap + row_tap
            windows_ref[:, LANES * index : LANES * index + LANES] = part.reshape(-1, LANES)
    terms = jnp.dot(act[...], windows_ref[...], preferred_element_type=F32) * factor
    pieces = [terms[:, LANES * index : LANES * index + 3 * OWN] for index in range(9)]
    pieces.append(jnp.zeros((channels, SLOT - TAPS * OWN), F32))
    terms = jnp.concatenate(pieces, axis=1)
    terms_ref[...] = terms.reshape(terms_ref.shape).astype(BF16)


def given(windows_ref, kernel_ref, give_ref, wide):
    chip, core = chip_and_core()
    bands, own_in, _ = kernel_ref.shape
    flat = kernel_ref[...].astype(F32).reshape(bands * own_in, SLOT)
    for index in range(9):
        wide[:, LANES * index : LANES * index + LANES] = flat[:, 3 * OWN * index : 3 * OWN * index + LANES].astype(BF16)
    for step in range(CHIPS):
        give_ref[step] = partial_of(windows_ref, wide, CORES * (chip ^ step) + 1 - core).astype(BF16)


def kept(windows_ref, wide_ref, keep_ref):
    chip, core = chip_and_core()
    for step in range(CHIPS):
        keep_ref[step] = partial_of(windows_ref, wide_ref, CORES * (chip ^ step) + core)


def partial_of(windows_ref, wide_ref, owner):
    rows = windows_ref[pl.ds(pl.multiple_of(LANES * owner, LANES), LANES)]
    return lax.dot_general(rows, wide_ref[...], (((1,), (1,)), ((), ())), preferred_element_type=F32)


def paired(keep_ref, given_ref, own_ref, *outs):
    own_ref[...] = keep_ref[0] + given_ref[0].astype(F32)
    for step, out in enumerate(outs, 1):
        out[...] = (keep_ref[step] + given_ref[step].astype(F32)).astype(BF16)


def finish(own_ref, first_ref, second_ref, third_ref, inputs_ref, cot_ref, out_ref):
    total = own_ref[...] + first_ref[...].astype(F32) + second_ref[...].astype(F32) + third_ref[...].astype(F32)
    total = total.reshape(inputs_ref.shape)
    values = inputs_ref[...].astype(F32)
    logistic = jax.nn.sigmoid(values)
    slope = logistic * (1.0 + values * (1.0 - logistic))
    out_ref[...] = (cot_ref[...].astype(F32) + total * slope).astype(BF16)


def summed(terms_ref, own_ref, other_ref):
    odd = lax.axis_index("rows") % 2
    own_ref[...] = jnp.sum(terms_ref[:, odd].astype(F32), axis=0)
    other_ref[...] = jnp.sum(terms_ref[:, 1 - odd].astype(F32), axis=0)


def total(own_ref, other_ref, out_ref):
    values = own_ref[...] + other_ref[...]
    for tap in range(TAPS):
        out_ref[tap] = values[:, OWN * tap : OWN * tap + OWN]


def stepped(block, step):
    count = GROUPS
    return lax.ppermute(block, "tm", [(i, i ^ step) for i in range(count)])


def near_and_far(bands):
    near = bands // FAR
    return (
        [[near * x + 2 * i + odd for i in range(near // 2)] for x in range(FAR) for odd in range(2)],
        [[near * x + i for x in range(FAR)] for i in range(near)],
    )


def alike(bands):
    return [[2 * i + odd for i in range(bands // 2)] for odd in range(2)]


def exchanged(blocks, groups):
    return lax.all_to_all(
        blocks, "rows", split_axis=0, concat_axis=0, tiled=True, axis_index_groups=groups
    )


def local(inputs, cotangent, kernel):
    frames, height, across, channels = inputs.shape
    bands = lax.axis_size("rows")
    own_in = kernel.shape[1]
    points = frames * height * across

    held = height * across
    swap, second, body = called(
        prepare,
        [
            array((4 * across + LANES // 4, LANES)), array((4 * across, LANES)),
            array((channels + CHIPS * held, LANES)),
        ],
        kernel, inputs, cotangent, limit=60,
    )
    first = lax.ppermute(swap, "rows", [(i, i ^ 1) for i in range(bands)])
    pairs = [(i, i + 1) for i in range(1, bands - 1, 2)]
    second = lax.ppermute(second, "rows", pairs + [(b, a) for a, b in pairs])
    blocks, = called(joined, [array((bands // FAR // 2, 2, own_in, SLOT))], swap, first)

    near, far = near_and_far(bands)
    blocks = exchanged(blocks, near)
    blocks = blocks.reshape(bands // FAR, own_in, SLOT)
    blocks = jnp.broadcast_to(blocks[None], (FAR, *blocks.shape))
    kernel_in = exchanged(blocks, far).reshape(bands, own_in, SLOT)

    span = (height + 2) * across
    payload = array((channels + span, LANES))
    packs = called(
        pack, [payload] * CHIPS, body, first, second,
        scratch=[pltpu.VMEM((CHIPS, 2 * across, LANES), BF16)],
    )
    packs = [packs[0]] + [stepped(packs[step], CORES * step) for step in range(1, CHIPS)]
    every = lax.all_gather(
        jnp.stack(packs), "tm", axis=0, axis_index_groups=PAIRS
    )

    factor = float(points * GROUPS * bands) ** (-0.5)

    def terms_body(*refs):
        windows_and_terms(factor, *refs)

    terms, windows = called(
        terms_body, [array((bands, own_in, SLOT)), array((GROUPS * points, WIDE))], every,
        scratch=[pltpu.VMEM((channels, GROUPS * points), BF16), pltpu.VMEM((frames * GROUPS + 2, span, LANES), BF16)],
        flops=2 * GROUPS * points * WIDE * channels,
    )
    terms = exchanged(terms.reshape(bands // 2, 2, own_in, SLOT), alike(bands))

    give, wide = called(
        given, [array((CHIPS, points, channels)), array((channels, WIDE))], windows, kernel_in,
        flops=GROUPS * points * WIDE * channels,
    )
    give = stepped(give, 1)
    keep, = called(
        kept, [array((CHIPS, points, channels), F32)], windows, wide,
        flops=GROUPS * points * WIDE * channels,
    )
    own, *sums = called(
        paired, [array((points, channels), F32)] + [array((points, channels))] * 3, keep, give
    )
    sums = [stepped(part, CORES * step) for step, part in enumerate(sums, 1)]
    mine, other = called(summed, [array((own_in, SLOT), F32)] * 2, terms)
    other = lax.ppermute(other, "rows", [(i, i ^ 1) for i in range(bands)])
    grad_inputs, = called(finish, [array(inputs.shape)], own, *sums, inputs, cotangent)
    grad_kernel, = called(total, [array(kernel.shape, F32)], mine, other)
    return (grad_inputs, grad_kernel)


def solution(mesh):
    return jax.shard_map(
        local,
        mesh=mesh,
        in_specs=(P("tm", "rows", None, None), P("tm", "rows", None, None), P(None, "rows", "tm")),
        out_specs=(P("tm", "rows", None, None), P(None, "rows", "tm")),
        check_vma=False,
    )
```

```python
import jax
import jax.numpy as jnp
from jax import lax
from jax.experimental import pallas as pl
from jax.experimental.pallas import tpu as pltpu
from jax.sharding import PartitionSpec as P


BF16 = jnp.bfloat16
F32 = jnp.float32
CHIPS = 4
CORES = 2
GROUPS = CHIPS * CORES
PAIRS = [[CORES * chip + core for core in range(CORES)] for chip in range(CHIPS)]
FAR = 4
OWN = 32
TAPS = 27
LANES = 128
SLOT = 896
WIDE = 9 * LANES


def chip_and_core():
    me = lax.axis_index("tm")
    return me // CORES, me % CORES


def called(body, outs, *args, scratch=(), flops=0, limit=24):
    whole = pl.BlockSpec(memory_space=pltpu.VMEM)
    size = sum(a.size * a.dtype.itemsize for a in (*args, *outs))
    return pl.pallas_call(
        body,
        out_shape=outs,
        in_specs=[whole] * len(args),
        out_specs=[whole] * len(outs),
        scratch_shapes=scratch,
        compiler_params=pltpu.CompilerParams(vmem_limit_bytes=limit << 20),
        cost_estimate=pl.CostEstimate(flops=flops, bytes_accessed=size, transcendentals=0),
    )(*args)


def array(shape, dtype=BF16):
    return jax.ShapeDtypeStruct(shape, dtype)


def prepare(kernel_ref, inputs_ref, cot_ref, swap_ref, second_ref, body_ref):
    own_in = kernel_ref.shape[1]
    across, channels = inputs_ref.shape[2:]
    odd = lax.axis_index("rows") % 2
    last = cot_ref.shape[1] - 1
    for ref, row in ((swap_ref, (1 - odd) * last), (second_ref, odd * last)):
        for frame in range(2):
            values = cot_ref[frame, row]
            for tile in range(2):
                start = across * (2 * frame + tile)
                ref[start : start + across] = values[:, LANES * tile : LANES * tile + LANES]
    pieces = [kernel_ref[tap].astype(F32) for tap in range(TAPS)]
    pieces.append(jnp.zeros((own_in, SLOT - TAPS * OWN), F32))
    slot = jnp.concatenate(pieces, axis=1)
    tiles = [slot[:, start : start + LANES] for start in range(0, SLOT, LANES)]
    tiles.append(jnp.zeros((swap_ref.shape[0] - 4 * across - SLOT // LANES * own_in, LANES), F32))
    swap_ref[4 * across :] = jnp.concatenate(tiles, axis=0).astype(BF16)
    body_ref[:channels] = jax.nn.silu(inputs_ref[...].reshape(-1, channels).astype(F32)).T.astype(BF16)
    halves = [cot_ref[frame].reshape(-1, channels).astype(F32) for frame in range(2)]
    for target in range(CHIPS):
        part = for_chip(target, halves[0], halves[1])
        body_ref[channels + part.shape[0] * target : channels + part.shape[0] * (target + 1)] = part


def joined(own_ref, swapped_ref, blocks_ref):
    own_in = blocks_ref.shape[2]
    start = own_ref.shape[0] - LANES // 4
    odd = lax.axis_index("rows") % 2
    for place, ref in ((odd, own_ref), (1 - odd, swapped_ref)):
        values = ref[start:].astype(F32)
        tiles = [values[own_in * tile : own_in * tile + own_in] for tile in range(SLOT // LANES)]
        slot = jnp.concatenate(tiles, axis=1).astype(BF16)
        for pair in range(blocks_ref.shape[0]):
            blocks_ref[pair, place] = slot


def for_chip(target, first, second):
    tile = slice(LANES * (target // 2), LANES * (target // 2) + LANES)
    return halved(target, first[:, tile], second[:, tile])


def halved(target, first, second):
    low = lax.broadcasted_iota(jnp.int32, first.shape, 1) < LANES // 2
    if target % 2 == 0:
        second = pltpu.roll(second, LANES // 2, 1)
    else:
        first = pltpu.roll(first, LANES // 2, 1)
    return jnp.where(low, first, second).astype(BF16)


def pack(body_ref, first_ref, second_ref, *out_and_scratch):
    outs, halo = out_and_scratch[:CHIPS], out_and_scratch[CHIPS]
    chip, _ = chip_and_core()
    across = 16
    rows = outs[0].shape[0] - 2 * across
    channels = 256
    held = rows - channels
    odd = lax.axis_index("rows") % 2
    for side, ref in ((1 - odd, first_ref), (odd, second_ref)):
        tiles = [ref[across * tile : across * tile + across].astype(F32) for tile in range(4)]
        for target in range(CHIPS):
            tile = target // 2
            part = halved(target, tiles[tile], tiles[2 + tile])
            halo[target, pl.ds(pl.multiple_of(across * side, across), across)] = part
    for step, out in enumerate(outs):
        out[:channels] = body_ref[:channels]
        start = pl.multiple_of(channels + held * (chip ^ step), held)
        out[channels:rows] = body_ref[pl.ds(start, held)]
        out[rows:] = halo[chip ^ step]


def windows_and_terms(factor, all_ref, terms_ref, windows_ref, act, padded):
    chip, core = chip_and_core()
    channels = act.shape[0]
    across = 16
    height = 4
    span = (height + 2) * across
    row = lax.broadcasted_iota(jnp.int32, (LANES, LANES), 0)
    lane = lax.broadcasted_iota(jnp.int32, (LANES, LANES), 1)
    place = lax.broadcasted_iota(jnp.int32, (span, LANES), 0) % across
    group = lax.broadcasted_iota(jnp.int32, (span, LANES), 1) // OWN
    padded[2 * GROUPS :] = jnp.zeros((2, span, LANES), BF16)
    for other in range(CORES):
        for step in range(CHIPS):
            owner = CORES * (chip ^ step) + other
            act[:, pl.ds(pl.multiple_of(owner * LANES, LANES), LANES)] = all_ref[other, step, :channels]
            block = all_ref[other, step, channels:]
            held = span - 2 * across
            block = jnp.concatenate([block[held : held + across], block[:held], block[held + across :]], axis=0)
            for frame in range(2):
                chosen = (row == 64 * frame + OWN * core + lane % OWN).astype(F32).astype(BF16)
                copies = jnp.dot(block, chosen, preferred_element_type=F32)
                after = jnp.where(place == across - 1, 0.0, pltpu.roll(copies, span - 1, 0))
                before = jnp.where(place == 0, 0.0, pltpu.roll(copies, 1, 0))
                joined = jnp.where(group == 0, after, jnp.where(group == 1, copies, before))
                joined = jnp.where(group == 3, 0.0, joined)
                padded[CORES * owner + frame] = joined.astype(BF16)
    for time_tap in range(3):
        for row_tap in range(3):
            part = padded[2 - time_tap : 2 - time_tap + 2 * GROUPS, across * (2 - row_tap) : across * (2 - row_tap + height)]
            index = 3 * time_tap + row_tap
            windows_ref[:, LANES * index : LANES * index + LANES] = part.reshape(-1, LANES)
    terms = jnp.dot(act[...], windows_ref[...], preferred_element_type=F32) * factor
    pieces = [terms[:, LANES * index : LANES * index + 3 * OWN] for index in range(9)]
    pieces.append(jnp.zeros((channels, SLOT - TAPS * OWN), F32))
    terms = jnp.concatenate(pieces, axis=1)
    terms_ref[...] = terms.reshape(terms_ref.shape).astype(BF16)


def transposed(windows_ref, kernel_ref, keep_ref, give_ref, wide, product):
    chip, core = chip_and_core()
    bands, own_in, _ = kernel_ref.shape
    flat = kernel_ref[...].astype(F32).reshape(bands * own_in, SLOT)
    for index in range(9):
        wide[:, LANES * index : LANES * index + LANES] = flat[:, 3 * OWN * index : 3 * OWN * index + LANES].astype(BF16)
    product[...] = lax.dot_general(
        windows_ref[...], wide[...], (((1,), (1,)), ((), ())), preferred_element_type=F32
    ).reshape(product.shape)
    for step in range(CHIPS):
        keep_ref[step] = product[CORES * (chip ^ step) + core]
        give_ref[step] = product[CORES * (chip ^ step) + 1 - core].astype(BF16)


def paired(keep_ref, given_ref, own_ref, *outs):
    _, core = chip_and_core()
    own_ref[...] = keep_ref[0] + given_ref[1 - core, 0].astype(F32)
    for step, out in enumerate(outs, 1):
        out[...] = (keep_ref[step] + given_ref[1 - core, step].astype(F32)).astype(BF16)


def finish(own_ref, first_ref, second_ref, third_ref, inputs_ref, cot_ref, out_ref):
    total = own_ref[...] + first_ref[...].astype(F32) + second_ref[...].astype(F32) + third_ref[...].astype(F32)
    total = total.reshape(inputs_ref.shape)
    values = inputs_ref[...].astype(F32)
    logistic = jax.nn.sigmoid(values)
    slope = logistic * (1.0 + values * (1.0 - logistic))
    out_ref[...] = (cot_ref[...].astype(F32) + total * slope).astype(BF16)


def summed(terms_ref, own_ref, other_ref):
    odd = lax.axis_index("rows") % 2
    own_ref[...] = jnp.sum(terms_ref[:, odd].astype(F32), axis=0)
    other_ref[...] = jnp.sum(terms_ref[:, 1 - odd].astype(F32), axis=0)


def total(own_ref, other_ref, out_ref):
    values = own_ref[...] + other_ref[...]
    for tap in range(TAPS):
        out_ref[tap] = values[:, OWN * tap : OWN * tap + OWN]


def stepped(block, step):
    count = GROUPS
    return lax.ppermute(block, "tm", [(i, i ^ step) for i in range(count)])


def near_and_far(bands):
    near = bands // FAR
    return (
        [[near * x + 2 * i + odd for i in range(near // 2)] for x in range(FAR) for odd in range(2)],
        [[near * x + i for x in range(FAR)] for i in range(near)],
    )


def alike(bands):
    return [[2 * i + odd for i in range(bands // 2)] for odd in range(2)]


def exchanged(blocks, groups):
    return lax.all_to_all(
        blocks, "rows", split_axis=0, concat_axis=0, tiled=True, axis_index_groups=groups
    )


def local(inputs, cotangent, kernel):
    frames, height, across, channels = inputs.shape
    bands = lax.axis_size("rows")
    own_in = kernel.shape[1]
    points = frames * height * across

    held = height * across
    swap, second, body = called(
        prepare,
        [
            array((4 * across + LANES // 4, LANES)), array((4 * across, LANES)),
            array((channels + CHIPS * held, LANES)),
        ],
        kernel, inputs, cotangent, limit=60,
    )
    first = lax.ppermute(swap, "rows", [(i, i ^ 1) for i in range(bands)])
    pairs = [(i, i + 1) for i in range(1, bands - 1, 2)]
    second = lax.ppermute(second, "rows", pairs + [(b, a) for a, b in pairs])
    blocks, = called(joined, [array((bands // FAR // 2, 2, own_in, SLOT))], swap, first)

    near, far = near_and_far(bands)
    blocks = exchanged(blocks, near)
    blocks = blocks.reshape(bands // FAR, own_in, SLOT)
    blocks = jnp.broadcast_to(blocks[None], (FAR, *blocks.shape))
    kernel_in = exchanged(blocks, far).reshape(bands, own_in, SLOT)

    span = (height + 2) * across
    payload = array((channels + span, LANES))
    packs = called(
        pack, [payload] * CHIPS, body, first, second,
        scratch=[pltpu.VMEM((CHIPS, 2 * across, LANES), BF16)],
    )
    packs = [packs[0]] + [stepped(packs[step], CORES * step) for step in range(1, CHIPS)]
    every = lax.all_gather(
        jnp.stack(packs), "tm", axis=0, axis_index_groups=PAIRS
    )

    factor = float(points * GROUPS * bands) ** (-0.5)

    def terms_body(*refs):
        windows_and_terms(factor, *refs)

    terms, windows = called(
        terms_body, [array((bands, own_in, SLOT)), array((GROUPS * points, WIDE))], every,
        scratch=[pltpu.VMEM((channels, GROUPS * points), BF16), pltpu.VMEM((frames * GROUPS + 2, span, LANES), BF16)],
        flops=2 * GROUPS * points * WIDE * channels,
    )
    terms = exchanged(terms.reshape(bands // 2, 2, own_in, SLOT), alike(bands))

    keep, give = called(
        transposed, [array((CHIPS, points, channels), F32), array((CHIPS, points, channels))],
        windows, kernel_in,
        scratch=[pltpu.VMEM((channels, WIDE), BF16), pltpu.VMEM((GROUPS, points, channels), F32)],
        flops=2 * GROUPS * points * WIDE * channels,
    )
    given = lax.all_gather(give, "tm", axis=0, axis_index_groups=PAIRS)
    own, *sums = called(
        paired, [array((points, channels), F32)] + [array((points, channels))] * 3, keep, given
    )
    sums = [stepped(part, CORES * step) for step, part in enumerate(sums, 1)]
    mine, other = called(summed, [array((own_in, SLOT), F32)] * 2, terms)
    other = lax.ppermute(other, "rows", [(i, i ^ 1) for i in range(bands)])
    grad_inputs, = called(finish, [array(inputs.shape)], own, *sums, inputs, cotangent)
    grad_kernel, = called(total, [array(kernel.shape, F32)], mine, other)
    return (grad_inputs, grad_kernel)


def solution(mesh):
    return jax.shard_map(
        local,
        mesh=mesh,
        in_specs=(P("tm", "rows", None, None), P("tm", "rows", None, None), P(None, "rows", "tm")),
        out_specs=(P("tm", "rows", None, None), P(None, "rows", "tm")),
        check_vma=False,
    )
```
